32 devices in a mesh: tm: 8 (over z, y), rep: 4 (over x, core).
Axes of the slice: x: 2, y: 2, z: 4, core: 2. Of those that a mesh axis runs over, the one named last changes fastest.
Arguments:
- transitions: float32 [32, 512, 512], P(('rep', 'tm')), parts along dimension 0, may hold values from -1 to 1, as said below
- cond_covs: float32 [32, 512, 512], P(('rep', 'tm')), parts along dimension 0, may hold values from -40 to 40, as said below
- transition_est: float32 [2048, 512], P('rep'), parts along dimension 0, may hold values from -0.25 to 0.25
Outputs:
- cov_blocks: float32 [32, 512, 512], P(('rep', 'tm')), parts along dimension 0
- transition_grad: float32 [2048, 512], P('rep'), parts along dimension 0
The draws below stay inside these ranges and needn't reach their ends.
There are 4 independent parts, one for each index of `rep`. The reference program is written for one: setup_inputs(seed, part) draws one part's arguments, and reference() takes and returns one part's arrays. A program takes and returns all parts, laid end to end along the dimension named above; each array names one. Nothing has to cross between parts.
Inputs may be any that keep to these rules, and one draw needn't show every extreme that they name: `transitions`: every block has spectral norm below one. `cond_covs`: every block is symmetric and positive definite.
All inputs are finite; a program needn't handle non-finite values.
Results may differ from the reference program's by a relative error of at most 0.00017.
Values sent between devices are 32-bit elements; how exact they have to be, the bound alone decides.
A program may use at most 192 MiB of HBM per device.

```python
import math
import jax
import jax.numpy as jnp
from jax import lax

S = 512
EPOCH_TOTAL = 8


def draw_transitions(key, part):
    stochastic_child_keys = jax.random.split(jax.random.fold_in(key, 11), 6)
    fast_share = 0.5
    forgetful = jax.random.uniform(stochastic_child_keys[0], (S,)) < fast_share
    lifetime = jnp.exp(jax.random.uniform(stochastic_child_keys[1], (S,), minval=0.0, maxval=math.log(4.0)))
    fast_retention = jnp.exp(-1.0 / lifetime)
    factor_block = jnp.exp(jax.random.uniform(stochastic_child_keys[2], (EPOCH_TOTAL, 1), minval=math.log(0.5), maxval=math.log(2.0)))
    slow_component_level = jax.random.uniform(stochastic_child_keys[3], (EPOCH_TOTAL, S), minval=0.3, maxval=1.0) * factor_block
    gradual_persistence_weight = 10.0 ** (-slow_component_level / (2.0 * EPOCH_TOTAL))
    perturbation_draws = jax.random.uniform(stochastic_child_keys[4], (EPOCH_TOTAL, 1)) < 3.0 / EPOCH_TOTAL
    gradual_persistence_weight = gradual_persistence_weight * jnp.where(perturbation_draws, 0.7, 1.0)
    persistence_weight = jnp.where(forgetful[None, :], fast_retention[None, :], gradual_persistence_weight)
    mixing = 1.5 * jnp.eye(S, dtype=jnp.float32)[None] + jax.random.normal(stochastic_child_keys[5], (EPOCH_TOTAL, S, S)) / math.sqrt(S)
    orthogonal, upper = jnp.linalg.qr(mixing)
    diagonal_sign = jnp.diagonal(upper, axis1=1, axis2=2)
    diagonal_sign = diagonal_sign / jnp.abs(diagonal_sign)
    orthogonal = orthogonal * diagonal_sign[:, None, :]
    return (persistence_weight[:, :, None] * orthogonal).astype(jnp.float32)


def draw_cond_covs(key, part):
    stochastic_child_keys = jax.random.split(jax.random.fold_in(key, 23), 2)
    factor = jnp.clip(jax.random.normal(stochastic_child_keys[0], (EPOCH_TOTAL, S, S)), -4.0, 4.0)
    wishart = jnp.einsum('bij,bkj->bik', factor, factor, precision=lax.Precision.HIGHEST) / S
    wishart = wishart + 0.5 * jnp.eye(S, dtype=jnp.float32)[None]
    scales = jnp.exp(jax.random.uniform(stochastic_child_keys[1], (EPOCH_TOTAL, S), minval=math.log(0.6), maxval=math.log(1.6)))
    result = scales[:, :, None] * wishart * scales[:, None, :] * (2.0 / math.sqrt(EPOCH_TOTAL))
    return result.astype(jnp.float32)


def scatter_about(key, extent, scale, reach, kind=jnp.bfloat16):
    values = jax.random.normal(key, extent, jnp.float32) * scale
    return jnp.minimum(jnp.maximum(values, -reach), reach).astype(kind)


def setup_inputs(seed: int = 0, part: int = 0) -> dict:
    keys = jax.random.split(jax.random.key(seed), 4)
    part_keys = jax.random.split(jax.random.fold_in(keys[3], part), 4)
    transitions = draw_transitions(jax.random.fold_in(jax.random.fold_in(keys[3], part), 71), part)
    cond_covs = draw_cond_covs(jax.random.fold_in(jax.random.fold_in(keys[3], part), 71), part)
    transition_est = scatter_about(part_keys[2], (S, S), S ** -0.5, 0.25, jnp.float32)
    return dict(transitions=transitions, cond_covs=cond_covs, transition_est=transition_est)


highest = lax.Precision.HIGHEST

def times_transposed(left, right):
    return lax.dot_general(left.astype(jnp.float32), right.astype(jnp.float32), (((1,), (1,)), ((), ())), precision=highest, preferred_element_type=jnp.float32)

def reference(transitions, cond_covs, transition_est):

    def backward_step(covariance, blocks):
        transition, conditional = blocks
        previous_step_cross = times_transposed(covariance, transition)
        current = jnp.dot(transition.astype(jnp.float32), previous_step_cross.astype(jnp.float32), precision=highest, preferred_element_type=jnp.float32) + conditional
        return (current, (current, previous_step_cross))
    empty_block = jnp.zeros((S, S), jnp.float32)
    last_cov, output_values = lax.scan(backward_step, empty_block, (transitions, cond_covs), reverse=True)
    covariances, laggeds = output_values
    lagged_sum = jnp.sum(laggeds[:-1], axis=0)
    variance_accumulator = jnp.sum(covariances[:-1], axis=0)
    gradient = (lagged_sum - jnp.dot(transition_est.astype(jnp.float32), variance_accumulator.astype(jnp.float32), precision=highest, preferred_element_type=jnp.float32)) / (EPOCH_TOTAL - 1)
    return (covariances, gradient)
```

```python
import functools

import jax
import jax.numpy as jnp
from jax import lax
from jax.experimental import pallas as pl
from jax.experimental.pallas import tpu as pltpu
from jax.sharding import PartitionSpec as P

CHUNKS = 4


def split(value):
    high = value.astype(jnp.bfloat16)
    low = (value - high.astype(jnp.float32)).astype(jnp.bfloat16)
    return high, low


def product(left, right, transposed=False):
    dims = (((1,), (1 if transposed else 0,)), ((), ()))

    def dot(a, b):
        return lax.dot_general(a, b, dims, preferred_element_type=jnp.float32)

    return dot(left[0], right[0]) + (dot(left[0], right[1]) + dot(left[1], right[0]))


def kernel(
    n, g_ref, c_ref, f_ref, cov_ref, grad_ref,
    g_in, c_in, c_odd, cov_in, grad_buf, sum_in, sum_out, d_half, k_half, s_half,
    ge, go, a, f, e, l_half,
    pair_send, pair_recv, down_send, down_recv, side_send, side_recv,
    sum_send, sum_recv, up_send, up_recv, share_send, share_recv,
):
    width = f_ref.shape[0]
    half = width // 2
    rows = width // CHUNKS
    me = lax.axis_index("tm")
    side, pair, pairs = me % 2, me // 2, n // 2
    is_even, is_odd = side == 0, side == 1
    partner, up, down = me + 1 - 2 * side, me + 2, me - 2
    has_up, has_down = pair < pairs - 1, pair > 0
    mine = pl.ds(pl.multiple_of(side * half, half), half)
    other = pl.ds(pl.multiple_of((1 - side) * half, half), half)

    def chunk(r):
        return pl.ds(r * rows, rows)

    def remote(src, dst, send, recv, device):
        return pltpu.make_async_remote_copy(
            src_ref=src, dst_ref=dst, send_sem=send, recv_sem=recv,
            device_id={"tm": device}, device_id_type=pl.DeviceIdType.MESH,
        )

    def get(pair_ref, *index):
        return pair_ref[(0, *index)], pair_ref[(1, *index)]

    def put(pair_ref, value, *index):
        high, low = split(value)
        pair_ref[(0, *index)] = high
        pair_ref[(1, *index)] = low

    every = slice(None)

    barrier = pltpu.get_barrier_semaphore()

    def greet(device):
        pl.semaphore_signal(
            barrier, inc=1, device_id={"tm": device}, device_id_type=pl.DeviceIdType.MESH
        )

    greet(partner)
    pl.when(has_up)(lambda: greet(up))
    pl.when(has_down)(lambda: greet(down))
    pl.semaphore_wait(barrier, 1 + has_up.astype(jnp.int32) + has_down.astype(jnp.int32))

    send_g = remote(g_ref.at[0], g_in, pair_send.at[0], pair_recv.at[0], partner)
    send_c = remote(c_ref.at[0], c_in, pair_send.at[1], pair_recv.at[1], partner)
    send_c_half = remote(
        c_ref.at[0, :, pl.ds(half, half)], c_in.at[:, pl.ds(half, half)],
        pair_send.at[1], pair_recv.at[1], partner,
    )

    @pl.when(is_odd)
    def _():
        send_c.start()
        send_g.start()

    @pl.when(is_even)
    def _():
        send_g.start()
        send_c_half.start()

    put(f, f_ref[...], every, every)

    @pl.when(is_even)
    def _():
        put(ge, g_ref[0], every, every)
        send_c.wait_recv()
        c_odd[...] = c_in[...]

    @pl.when(is_odd)
    def _():
        c_odd[...] = c_ref[0]
        put(go, g_ref[0], every, every)
        send_g.wait_recv()
        put(ge, g_in[...], every, every)

    k_value = product(split(c_odd[...]), get(ge, mine, every), True)
    k_half[...] = k_value
    d_half[...] = product(get(ge, every, every), split(k_value))

    @pl.when(is_even)
    def _():
        d_half[...] += c_ref[0, :, :half]

    @pl.when(is_odd)
    def _():
        send_c_half.wait_recv()
        d_half[...] += c_in[:, half:]

    def send_down(r):
        return remote(
            s_half.at[chunk(r)], cov_in.at[side, chunk(r)], down_send.at[r], down_recv.at[r], down
        )

    def send_side(r):
        return remote(
            cov_in.at[side, chunk(r)], cov_in.at[side, chunk(r)],
            side_send.at[r], side_recv.at[r], partner,
        )

    @pl.when(jnp.logical_not(has_up))
    def _():
        s_half[...] = d_half[...]
        for r in range(CHUNKS):
            pl.when(has_down)(send_down(r).start)

    @pl.when(is_even)
    def _():
        send_g.wait_recv()
        put(go, g_in[...], every, every)

    @pl.when(jnp.logical_not(has_up))
    def _():
        e[...] = jnp.zeros_like(e)
        l_half[...] = jnp.zeros_like(l_half)

    @pl.when(has_up)
    def _():
        put(a, product(get(ge, every, every), get(go, every, every)), every, every)
        for r in range(CHUNKS + 1):
            if r < CHUNKS:
                send_down(r).wait_recv()
                send_side(r).start()
            if r > 0:
                q = chunk(r - 1)
                send_side(r - 1).wait_recv()
                put(e, cov_in[0, q], q, slice(0, half))
                put(e, cov_in[1, q], q, slice(half, width))
                put(l_half, product(get(e, q, every), get(a, mine, every), True), q, every)
        for r in range(CHUNKS):
            q = chunk(r)
            s_half[q] = product(get(a, q, every), get(l_half, every, every)) + d_half[q]
            pl.when(has_down)(send_down(r).start)

    lag_odd = product(get(e, every, every), get(go, mine, every), True)
    sigma_odd = product(get(go, every, every), split(lag_odd))

    @pl.when(is_even)
    def _():
        sum_out[...] = sigma_odd + c_odd[:, :half]

    @pl.when(is_odd)
    def _():
        own = sigma_odd + c_odd[:, half:]
        sum_out[...] = own
        cov_ref[0, :, half:] = own

    counted = jnp.where(has_up, 1.0, 0.0).astype(jnp.float32)
    variance = counted * sum_out[...] + s_half[...]
    terms = (
        lag_odd
        + (product(get(go, every, every), get(l_half, every, every)) + k_half[...])
        - product(get(f, every, every), split(variance))
    )
    send_sum = remote(sum_out, sum_in, sum_send, sum_recv, down)
    sum_out[...] = terms

    @pl.when(has_up)
    def _():
        send_sum.wait_recv()
        sum_out[...] += sum_in[...]

    pl.when(has_down)(send_sum.start)

    def send_up(r):
        return remote(
            grad_buf.at[side, chunk(r)], grad_buf.at[side, chunk(r)],
            up_send.at[r], up_recv.at[r], up,
        )

    def share(r):
        return remote(
            grad_buf.at[side, chunk(r)], grad_buf.at[side, chunk(r)],
            share_send.at[r], share_recv.at[r], partner,
        )

    @pl.when(jnp.logical_not(has_down))
    def _():
        grad_buf[side] = sum_out[...] / (n - 1)
        for r in range(CHUNKS):
            pl.when(has_up)(send_up(r).start)
            share(r).start()

    @pl.when(is_even)
    def _():
        cov_ref[0, :, :half] = s_half[...]
        k_other = product(split(c_odd[...]), get(ge, other, every), True)
        cov_ref[0, :, half:] = (
            product(get(ge, every, every), split(k_other)) + c_ref[0, :, half:]
        )

        @pl.when(has_up)
        def _():
            l_other = product(get(e, every, every), get(a, other, every), True)
            cov_ref[0, :, half:] += product(get(a, every, every), split(l_other))

    @pl.when(is_odd)
    def _():
        l_other = product(get(e, every, every), get(go, other, every), True)
        cov_ref[0, :, :half] = (
            product(get(go, every, every), split(l_other)) + c_odd[:, :half]
        )

    @pl.when(has_down)
    def _():
        for r in range(CHUNKS):
            send_up(r).wait_recv()
            pl.when(has_up)(send_up(r).start)
            share(r).start()

    for r in range(CHUNKS):
        share(r).wait_recv()
        grad_ref[chunk(r), :half] = grad_buf[0, chunk(r)]
        grad_ref[chunk(r), half:] = grad_buf[1, chunk(r)]

    send_g.wait_send()
    pl.when(is_odd)(send_c.wait_send)
    pl.when(is_even)(send_c_half.wait_send)
    pl.when(has_down)(send_sum.wait_send)
    for r in range(CHUNKS):
        pl.when(has_down)(send_down(r).wait_send)
        pl.when(has_up)(send_side(r).wait_send)
        pl.when(has_up)(send_up(r).wait_send)
        share(r).wait_send()


def on_device(n, transitions, cond_covs, transition_est):
    width = transitions.shape[1]
    half = width // 2
    f32, b16 = jnp.float32, jnp.bfloat16
    vmem = pl.BlockSpec(memory_space=pltpu.VMEM)
    whole, column_half = (width, width), (width, half)
    dma = pltpu.SemaphoreType.DMA
    return pl.pallas_call(
        functools.partial(kernel, n),
        out_shape=(
            jax.ShapeDtypeStruct(transitions.shape, f32),
            jax.ShapeDtypeStruct(transition_est.shape, f32),
        ),
        in_specs=[vmem] * 3,
        out_specs=(vmem, vmem),
        scratch_shapes=[
            pltpu.VMEM(whole, f32),
            pltpu.VMEM(whole, f32),
            pltpu.VMEM(whole, f32),
            pltpu.VMEM((2, *column_half), f32),
            pltpu.VMEM((2, *column_half), f32),
            pltpu.VMEM(column_half, f32),
            pltpu.VMEM(column_half, f32),
            pltpu.VMEM(column_half, f32),
            pltpu.VMEM(column_half, f32),
            pltpu.VMEM(column_half, f32),
            pltpu.VMEM((2, *whole), b16),
            pltpu.VMEM((2, *whole), b16),
            pltpu.VMEM((2, *whole), b16),
            pltpu.VMEM((2, *whole), b16),
            pltpu.VMEM((2, *whole), b16),
            pltpu.VMEM((2, *column_half), b16),
            dma((2,)), dma((2,)),
            dma((CHUNKS,)), dma((CHUNKS,)), dma((CHUNKS,)), dma((CHUNKS,)),
            dma, dma,
            dma((CHUNKS,)), dma((CHUNKS,)), dma((CHUNKS,)), dma((CHUNKS,)),
        ],
        compiler_params=pltpu.CompilerParams(
            collective_id=0, has_side_effects=True, vmem_limit_bytes=56 * 2**20
        ),
    )(transitions, cond_covs, transition_est)


def solution(mesh):
    return jax.shard_map(
        functools.partial(on_device, mesh.shape["tm"]),
        mesh=mesh,
        in_specs=(P(("rep", "tm"), None, None), P(("rep", "tm"), None, None), P("rep", None)),
        out_specs=(P(("rep", "tm"), None, None), P("rep", None)),
        check_vma=False,
    )
```

```python
import functools

import jax
import jax.numpy as jnp
from jax import lax
from jax.experimental import pallas as pl
from jax.experimental.pallas import tpu as pltpu
from jax.sharding import PartitionSpec as P

CHUNKS = 4
PIECES = 2


def split(value):
    high = value.astype(jnp.bfloat16)
    low = (value - high.astype(jnp.float32)).astype(jnp.bfloat16)
    return high, low


def product(left, right, transposed=False):
    dims = (((1,), (1 if transposed else 0,)), ((), ()))

    def dot(a, b):
        return lax.dot_general(a, b, dims, preferred_element_type=jnp.float32)

    return dot(left[0], right[0]) + (dot(left[0], right[1]) + dot(left[1], right[0]))


def kernel(
    n, g_ref, c_ref, f_ref, cov_ref, grad_ref,
    g_in, c_in, c_odd, cov_in, grad_buf, sum_in, sum_out, d_half, k_half, s_half,
    lag_odd, sigma_odd, ge, go, a, f, e, l_half, v_half,
    pair_send, pair_recv, down_send, down_recv, side_send, side_recv,
    sum_send, sum_recv, up_send, up_recv, share_send, share_recv,
):
    width = f_ref.shape[0]
    half = width // 2
    rows = width // CHUNKS
    me = lax.axis_index("tm")
    side, pair, pairs = me % 2, me // 2, n // 2
    is_even, is_odd = side == 0, side == 1
    partner, up, down = me + 1 - 2 * side, me + 2, me - 2
    has_up, has_down = pair < pairs - 1, pair > 0
    mine = pl.ds(pl.multiple_of(side * half, half), half)
    other = pl.ds(pl.multiple_of((1 - side) * half, half), half)

    def chunk(r):
        return pl.ds(r * rows, rows)

    sends = CHUNKS * PIECES

    def piece(t):
        return pl.ds(t * (width // sends), width // sends)

    def pieces(r):
        return range(r * PIECES, (r + 1) * PIECES)

    def remote(src, dst, send, recv, device):
        return pltpu.make_async_remote_copy(
            src_ref=src, dst_ref=dst, send_sem=send, recv_sem=recv,
            device_id={"tm": device}, device_id_type=pl.DeviceIdType.MESH,
        )

    def get(pair_ref, *index):
        return pair_ref[(0, *index)], pair_ref[(1, *index)]

    def put(pair_ref, value, *index):
        high, low = split(value)
        pair_ref[(0, *index)] = high
        pair_ref[(1, *index)] = low

    every = slice(None)

    barrier = pltpu.get_barrier_semaphore()

    def greet(device):
        pl.semaphore_signal(
            barrier, inc=1, device_id={"tm": device}, device_id_type=pl.DeviceIdType.MESH
        )

    greet(partner)
    pl.when(has_up)(lambda: greet(up))
    pl.when(has_down)(lambda: greet(down))
    pl.semaphore_wait(barrier, 1 + has_up.astype(jnp.int32) + has_down.astype(jnp.int32))

    send_g = remote(g_ref.at[0], g_in, pair_send.at[0], pair_recv.at[0], partner)
    send_c = remote(c_ref.at[0], c_in, pair_send.at[1], pair_recv.at[1], partner)
    send_c_half = remote(
        c_ref.at[0, :, pl.ds(half, half)], c_in.at[:, pl.ds(half, half)],
        pair_send.at[1], pair_recv.at[1], partner,
    )

    @pl.when(is_odd)
    def _():
        send_c.start()
        send_g.start()

    @pl.when(is_even)
    def _():
        send_g.start()
        send_c_half.start()

    put(f, f_ref[...], every, every)

    @pl.when(is_even)
    def _():
        put(ge, g_ref[0], every, every)
        send_c.wait_recv()
        c_odd[...] = c_in[...]

    @pl.when(is_odd)
    def _():
        c_odd[...] = c_ref[0]
        put(go, g_ref[0], every, every)
        send_g.wait_recv()
        put(ge, g_in[...], every, every)

    k_value = product(split(c_odd[...]), get(ge, mine, every), True)
    k_half[...] = k_value
    d_half[...] = product(get(ge, every, every), split(k_value))

    @pl.when(is_even)
    def _():
        d_half[...] += c_ref[0, :, :half]

    @pl.when(is_odd)
    def _():
        send_c_half.wait_recv()
        d_half[...] += c_in[:, half:]

    def send_down(r):
        return remote(
            s_half.at[piece(r)], cov_in.at[side, piece(r)], down_send.at[r], down_recv.at[r], down
        )

    def send_side(r):
        return remote(
            cov_in.at[side, piece(r)], cov_in.at[side, piece(r)],
            side_send.at[r], side_recv.at[r], partner,
        )

    @pl.when(jnp.logical_not(has_up))
    def _():
        s_half[...] = d_half[...]
        for r in range(sends):
            pl.when(has_down)(send_down(r).start)

    @pl.when(is_even)
    def _():
        send_g.wait_recv()
        put(go, g_in[...], every, every)

    @pl.when(jnp.logical_not(has_up))
    def _():
        e[...] = jnp.zeros_like(e)
        l_half[...] = jnp.zeros_like(l_half)
        lag_odd[...] = jnp.zeros_like(lag_odd)

    @pl.when(has_up)
    def _():
        put(a, product(get(ge, every, every), get(go, every, every)), every, every)
        for t in range(sends + 1):
            if t < sends:
                send_down(t).wait_recv()
                send_side(t).start()
            if t > 0:
                send_side(t - 1).wait_recv()
                if t % PIECES == 0:
                    q = chunk(t // PIECES - 1)
                    put(e, cov_in[0, q], q, slice(0, half))
                    put(e, cov_in[1, q], q, slice(half, width))
                    rows_of_e = get(e, q, every)
                    put(l_half, product(rows_of_e, get(a, mine, every), True), q, every)
                    lag_odd[q] = product(rows_of_e, get(go, mine, every), True)
        for r in range(CHUNKS):
            q = chunk(r)
            s_half[q] = product(get(a, q, every), get(l_half, every, every)) + d_half[q]
            for t in pieces(r):
                pl.when(has_down)(send_down(t).start)

    sigma_odd[...] = product(get(go, every, every), split(lag_odd[...]))

    @pl.when(is_even)
    def _():
        sigma_odd[...] += c_odd[:, :half]

    @pl.when(is_odd)
    def _():
        own = sigma_odd[...] + c_odd[:, half:]
        sigma_odd[...] = own
        cov_ref[0, :, half:] = own

    counted = jnp.where(has_up, 1.0, 0.0).astype(jnp.float32)
    put(v_half, counted * sigma_odd[...] + s_half[...], every, every)

    def send_sum(r):
        return remote(
            sum_out.at[chunk(r)], sum_in.at[chunk(r)], sum_send.at[r], sum_recv.at[r], down
        )

    def send_up(r):
        return remote(
            grad_buf.at[side, piece(r)], grad_buf.at[side, piece(r)],
            up_send.at[r], up_recv.at[r], up,
        )

    def share(r):
        return remote(
            grad_buf.at[side, piece(r)], grad_buf.at[side, piece(r)],
            share_send.at[r], share_recv.at[r], partner,
        )

    for r in range(CHUNKS):
        q = chunk(r)
        sum_out[q] = (
            lag_odd[q]
            + (product(get(go, q, every), get(l_half, every, every)) + k_half[q])
            - product(get(f, q, every), get(v_half, every, every))
        )

        @pl.when(has_up)
        def _():
            send_sum(r).wait_recv()
            sum_out[q] += sum_in[q]

        pl.when(has_down)(send_sum(r).start)

        @pl.when(jnp.logical_not(has_down))
        def _():
            grad_buf[side, q] = sum_out[q] / (n - 1)
            for t in pieces(r):
                pl.when(has_up)(send_up(t).start)
                share(t).start()

    @pl.when(is_even)
    def _():
        cov_ref[0, :, :half] = s_half[...]
        k_other = product(split(c_odd[...]), get(ge, other, every), True)
        cov_ref[0, :, half:] = (
            product(get(ge, every, every), split(k_other)) + c_ref[0, :, half:]
        )

        @pl.when(has_up)
        def _():
            l_other = product(get(e, every, every), get(a, other, every), True)
            cov_ref[0, :, half:] += product(get(a, every, every), split(l_other))

    @pl.when(is_odd)
    def _():
        l_other = product(get(e, every, every), get(go, other, every), True)
        cov_ref[0, :, :half] = (
            product(get(go, every, every), split(l_other)) + c_odd[:, :half]
        )

    @pl.when(has_down)
    def _():
        for r in range(sends):
            send_up(r).wait_recv()
            pl.when(has_up)(send_up(r).start)
            share(r).start()

    for r in range(sends):
        share(r).wait_recv()
        grad_ref[piece(r), :half] = grad_buf[0, piece(r)]
        grad_ref[piece(r), half:] = grad_buf[1, piece(r)]

    send_g.wait_send()
    pl.when(is_odd)(send_c.wait_send)
    pl.when(is_even)(send_c_half.wait_send)
    for r in range(CHUNKS):
        pl.when(has_down)(send_sum(r).wait_send)
    for r in range(sends):
        pl.when(has_down)(send_down(r).wait_send)
        pl.when(has_up)(send_side(r).wait_send)
        pl.when(has_up)(send_up(r).wait_send)
        share(r).wait_send()


def on_device(n, transitions, cond_covs, transition_est):
    width = transitions.shape[1]
    half = width // 2
    f32, b16 = jnp.float32, jnp.bfloat16
    vmem = pl.BlockSpec(memory_space=pltpu.VMEM)
    whole, column_half = (width, width), (width, half)
    dma = pltpu.SemaphoreType.DMA
    sends = CHUNKS * PIECES
    return pl.pallas_call(
        functools.partial(kernel, n),
        out_shape=(
            jax.ShapeDtypeStruct(transitions.shape, f32),
            jax.ShapeDtypeStruct(transition_est.shape, f32),
        ),
        in_specs=[vmem] * 3,
        out_specs=(vmem, vmem),
        scratch_shapes=[
            *[pltpu.VMEM(whole, f32)] * 3,
            *[pltpu.VMEM((2, *column_half), f32)] * 2,
            *[pltpu.VMEM(column_half, f32)] * 7,
            *[pltpu.VMEM((2, *whole), b16)] * 5,
            *[pltpu.VMEM((2, *column_half), b16)] * 2,
            *[dma((2,))] * 2,
            *[dma((sends,))] * 4,
            *[dma((CHUNKS,))] * 2,
            *[dma((sends,))] * 4,
        ],
        compiler_params=pltpu.CompilerParams(
            collective_id=0, has_side_effects=True, vmem_limit_bytes=56 * 2**20
        ),
    )(transitions, cond_covs, transition_est)


def solution(mesh):
    return jax.shard_map(
        functools.partial(on_device, mesh.shape["tm"]),
        mesh=mesh,
        in_specs=(P(("rep", "tm"), None, None), P(("rep", "tm"), None, None), P("rep", None)),
        out_specs=(P(("rep", "tm"), None, None), P("rep", None)),
        check_vma=False,
    )
```

```python
import functools

import jax
import jax.numpy as jnp
from jax import lax
from jax.experimental import pallas as pl
from jax.experimental.pallas import tpu as pltpu
from jax.sharding import PartitionSpec as P

CHUNKS = 4
PIECES = 2


def split(value):
    high = value.astype(jnp.bfloat16)
    low = (value - high.astype(jnp.float32)).astype(jnp.bfloat16)
    return high, low


def product(left, right, transposed=False):
    dims = (((1,), (1 if transposed else 0,)), ((), ()))

    def dot(a, b):
        return lax.dot_general(a, b, dims, preferred_element_type=jnp.float32)

    return dot(left[0], right[0]) + (dot(left[0], right[1]) + dot(left[1], right[0]))


def kernel(
    n, g_ref, c_ref, f_ref, cov_ref, grad_ref,
    g_in, c_in, c_odd, cov_in, grad_buf, sum_in, sum_out, d_half, k_half, s_half,
    lag_odd, sigma_odd, ge, go, a, f, e, l_half, v_half,
    pair_send, pair_recv, top_send, top_recv, down_send, down_recv, side_send, side_recv,
    sum_send, sum_recv, up_send, up_recv, share_send, share_recv,
):
    width = f_ref.shape[0]
    half = width // 2
    rows = width // CHUNKS
    me = lax.axis_index("tm")
    side, pair, pairs = me % 2, me // 2, n // 2
    is_even, is_odd = side == 0, side == 1
    partner, up, down = me + 1 - 2 * side, me + 2, me - 2
    has_up, has_down = pair < pairs - 1, pair > 0
    mine = pl.ds(pl.multiple_of(side * half, half), half)
    other = pl.ds(pl.multiple_of((1 - side) * half, half), half)

    def chunk(r):
        return pl.ds(r * rows, rows)

    sends = CHUNKS * PIECES

    def piece(t):
        return pl.ds(t * (width // sends), width // sends)

    def pieces(r):
        return range(r * PIECES, (r + 1) * PIECES)

    def remote(src, dst, send, recv, device):
        return pltpu.make_async_remote_copy(
            src_ref=src, dst_ref=dst, send_sem=send, recv_sem=recv,
            device_id={"tm": device}, device_id_type=pl.DeviceIdType.MESH,
        )

    def get(pair_ref, *index):
        return pair_ref[(0, *index)], pair_ref[(1, *index)]

    def put(pair_ref, value, *index):
        high, low = split(value)
        pair_ref[(0, *index)] = high
        pair_ref[(1, *index)] = low

    every = slice(None)

    barrier = pltpu.get_barrier_semaphore()

    def greet(device):
        pl.semaphore_signal(
            barrier, inc=1, device_id={"tm": device}, device_id_type=pl.DeviceIdType.MESH
        )

    greet(partner)
    pl.when(has_up)(lambda: greet(up))
    pl.when(has_down)(lambda: greet(down))
    pl.semaphore_wait(barrier, 1 + has_up.astype(jnp.int32) + has_down.astype(jnp.int32))

    is_top = jnp.logical_not(has_up)
    low, high = pl.ds(0, half), pl.ds(half, half)

    def swap(i, ref, target, *index):
        return remote(
            ref.at[(0, *index)], target.at[index], pair_send.at[i], pair_recv.at[i], partner
        )

    send_g = remote(g_ref.at[0], g_in, pair_send.at[0], pair_recv.at[0], partner)
    send_c_low = swap(1, c_ref, c_in, low)
    send_c_high = swap(2, c_ref, c_in, high, high)
    send_c_half = swap(1, c_ref, c_in, every, high)

    @pl.when(is_odd)
    def _():
        pl.when(has_up)(send_g.start)
        send_c_low.start()
        send_c_high.start()

    @pl.when(is_even & has_up)
    def _():
        send_g.start()
        send_c_half.start()

    def receive_c_odd():
        send_c_low.wait_recv()
        send_c_high.wait_recv()
        c_odd[low] = c_in[low]
        c_odd[high, half:] = c_in[high, half:]
        c_odd[high, :half] = c_in[low, half:].T

    def send_down(t):
        return remote(
            s_half.at[piece(t)], cov_in.at[side, piece(t)], down_send.at[t], down_recv.at[t], down
        )

    def send_side(t):
        return remote(
            cov_in.at[side, piece(t)], cov_in.at[side, piece(t)],
            side_send.at[t], side_recv.at[t], partner,
        )

    forwards = is_even | (pair < pairs - 2)

    def send_top(t):
        return remote(
            d_half.at[piece(t)], s_half.at[piece(t)], top_send.at[t], top_recv.at[t], partner
        )

    def send_other_down(t):
        return remote(
            d_half.at[piece(t)], cov_in.at[1, piece(t)], side_send.at[t], side_recv.at[t], down
        )

    @pl.when(is_even)
    def _():
        put(ge, g_ref[0], every, every)

    @pl.when(is_odd)
    def _():
        c_odd[...] = c_ref[0]

    @pl.when(is_top)
    def _():
        e[...] = jnp.zeros_like(e)
        go[...] = jnp.zeros_like(go)
        l_half[...] = jnp.zeros_like(l_half)
        lag_odd[...] = jnp.zeros_like(lag_odd)

    @pl.when(is_top & is_even)
    def _():
        receive_c_odd()
        k_all = product(split(c_odd[...]), get(ge, every, every), True)
        k_half[...] = k_all[:, :half]
        put(e, k_all, every, every)
        for r in range(CHUNKS):
            q = chunk(r)
            sigma = product(get(ge, q, every), get(e, every, every)) + c_ref[0, q]
            s_half[q] = sigma[:, :half]
            d_half[q] = sigma[:, half:]
            for t in pieces(r):
                send_top(t).start()
                pl.when(has_down)(send_down(t).start)
                pl.when(has_down)(send_other_down(t).start)
        send_g.start()
        e[...] = jnp.zeros_like(e)

    put(f, f_ref[...], every, every)

    @pl.when(is_top & is_odd)
    def _():
        for t in range(sends):
            send_top(t).wait_recv()
            pl.when(has_down)(send_down(t).start)
        send_g.wait_recv()
        put(ge, g_in[...], every, every)
        k_half[...] = product(split(c_odd[...]), get(ge, mine, every), True)

    @pl.when(has_up)
    def _():
        @pl.when(is_even)
        def _():
            send_g.wait_recv()
            put(go, g_in[...], every, every)

        @pl.when(is_odd)
        def _():
            put(go, g_ref[0], every, every)
            send_g.wait_recv()
            put(ge, g_in[...], every, every)

        put(a, product(get(ge, every, every), get(go, every, every)), every, every)
        pl.when(is_even)(receive_c_odd)
        k_value = product(split(c_odd[...]), get(ge, mine, every), True)
        k_half[...] = k_value
        d_half[...] = product(get(ge, every, every), split(k_value))

        @pl.when(is_even)
        def _():
            d_half[...] += c_ref[0, :, :half]

        @pl.when(is_odd)
        def _():
            send_c_half.wait_recv()
            d_half[...] += c_in[:, half:]

        def use(r):
            q = chunk(r)
            for t in pieces(r):
                send_side(t).wait_recv()
            put(e, cov_in[0, q], q, slice(0, half))
            put(e, cov_in[1, q], q, slice(half, width))
            rows_of_e = get(e, q, every)
            put(l_half, product(rows_of_e, get(a, mine, every), True), q, every)

            @pl.when(jnp.logical_not(has_down))
            def _():
                lag_odd[q] = product(rows_of_e, get(go, mine, every), True)

        used = 0
        for t in range(sends):
            send_down(t).wait_recv()
            pl.when(forwards)(send_side(t).start)
            if t % PIECES == 0 and t >= 2 * PIECES:
                use(used)
                used += 1
        for r in range(used, CHUNKS):
            use(r)
        for r in range(CHUNKS):
            q = chunk(r)
            s_half[q] = product(get(a, q, every), get(l_half, every, every)) + d_half[q]
            for t in pieces(r):
                pl.when(has_down)(send_down(t).start)

        @pl.when(has_down)
        def _():
            lag_odd[...] = product(get(e, every, every), get(go, mine, every), True)

    sigma_odd[...] = product(get(go, every, every), split(lag_odd[...]))

    @pl.when(is_even)
    def _():
        sigma_odd[...] += c_odd[:, :half]

    @pl.when(is_odd)
    def _():
        own = sigma_odd[...] + c_odd[:, half:]
        sigma_odd[...] = own
        cov_ref[0, :, half:] = own

    counted = jnp.where(has_up, 1.0, 0.0).astype(jnp.float32)
    put(v_half, counted * sigma_odd[...] + s_half[...], every, every)

    def send_sum(r):
        return remote(
            sum_out.at[chunk(r)], sum_in.at[chunk(r)], sum_send.at[r], sum_recv.at[r], down
        )

    def send_up(r):
        return remote(
            grad_buf.at[side, piece(r)], grad_buf.at[side, piece(r)],
            up_send.at[r], up_recv.at[r], up,
        )

    def share(r):
        return remote(
            grad_buf.at[side, piece(r)], grad_buf.at[side, piece(r)],
            share_send.at[r], share_recv.at[r], partner,
        )

    for r in range(CHUNKS):
        q = chunk(r)
        sum_out[q] = (
            lag_odd[q]
            + (product(get(go, q, every), get(l_half, every, every)) + k_half[q])
            - product(get(f, q, every), get(v_half, every, every))
        )

        @pl.when(has_up)
        def _():
            send_sum(r).wait_recv()
            sum_out[q] += sum_in[q]

        pl.when(has_down)(send_sum(r).start)

        @pl.when(jnp.logical_not(has_down))
        def _():
            grad_buf[side, q] = sum_out[q] / (n - 1)
            for t in pieces(r):
                pl.when(has_up)(send_up(t).start)
                share(t).start()

    @pl.when(is_even)
    def _():
        cov_ref[0, :, :half] = s_half[...]
        k_other = product(split(c_odd[...]), get(ge, other, every), True)
        cov_ref[0, :, half:] = (
            product(get(ge, every, every), split(k_other)) + c_ref[0, :, half:]
        )

        @pl.when(has_up)
        def _():
            l_other = product(get(e, every, every), get(a, other, every), True)
            cov_ref[0, :, half:] += product(get(a, every, every), split(l_other))

    @pl.when(is_odd)
    def _():
        l_other = product(get(e, every, every), get(go, other, every), True)
        cov_ref[0, :, :half] = (
            product(get(go, every, every), split(l_other)) + c_odd[:, :half]
        )

    @pl.when(has_down)
    def _():
        for r in range(sends):
            send_up(r).wait_recv()
            pl.when(has_up)(send_up(r).start)
            share(r).start()

    for r in range(sends):
        share(r).wait_recv()
        grad_ref[piece(r), :half] = grad_buf[0, piece(r)]
        grad_ref[piece(r), half:] = grad_buf[1, piece(r)]

    pl.when(has_up | is_even)(send_g.wait_send)
    pl.when(is_odd)(send_c_low.wait_send)
    pl.when(is_odd)(send_c_high.wait_send)
    pl.when(has_up & is_even)(send_c_half.wait_send)
    for r in range(CHUNKS):
        pl.when(has_down)(send_sum(r).wait_send)
    for r in range(sends):
        pl.when(has_down)(send_down(r).wait_send)
        pl.when(has_up & forwards)(send_side(r).wait_send)
        pl.when(is_top & is_even)(send_top(r).wait_send)
        pl.when(is_top & is_even & has_down)(send_other_down(r).wait_send)
        pl.when(has_up)(send_up(r).wait_send)
        share(r).wait_send()


def on_device(n, transitions, cond_covs, transition_est):
    width = transitions.shape[1]
    half = width // 2
    f32, b16 = jnp.float32, jnp.bfloat16
    vmem = pl.BlockSpec(memory_space=pltpu.VMEM)
    whole, column_half = (width, width), (width, half)
    dma = pltpu.SemaphoreType.DMA
    sends = CHUNKS * PIECES
    return pl.pallas_call(
        functools.partial(kernel, n),
        out_shape=(
            jax.ShapeDtypeStruct(transitions.shape, f32),
            jax.ShapeDtypeStruct(transition_est.shape, f32),
        ),
        in_specs=[vmem] * 3,
        out_specs=(vmem, vmem),
        scratch_shapes=[
            *[pltpu.VMEM(whole, f32)] * 3,
            *[pltpu.VMEM((2, *column_half), f32)] * 2,
            *[pltpu.VMEM(column_half, f32)] * 7,
            *[pltpu.VMEM((2, *whole), b16)] * 5,
            *[pltpu.VMEM((2, *column_half), b16)] * 2,
            *[dma((3,))] * 2,
            *[dma((sends,))] * 6,
            *[dma((CHUNKS,))] * 2,
            *[dma((sends,))] * 4,
        ],
        compiler_params=pltpu.CompilerParams(
            collective_id=0, has_side_effects=True, vmem_limit_bytes=56 * 2**20
        ),
    )(transitions, cond_covs, transition_est)


def solution(mesh):
    return jax.shard_map(
        functools.partial(on_device, mesh.shape["tm"]),
        mesh=mesh,
        in_specs=(P(("rep", "tm"), None, None), P(("rep", "tm"), None, None), P("rep", None)),
        out_specs=(P(("rep", "tm"), None, None), P("rep", None)),
        check_vma=False,
    )
```

```python
import functools

import jax
import jax.numpy as jnp
from jax import lax
from jax.experimental import pallas as pl
from jax.experimental.pallas import tpu as pltpu
from jax.sharding import PartitionSpec as P

CHUNKS = 4
PIECES = 4


def split(value):
    high = value.astype(jnp.bfloat16)
    low = (value - high.astype(jnp.float32)).astype(jnp.bfloat16)
    return high, low


def product(left, right, transposed=False):
    dims = (((1,), (1 if transposed else 0,)), ((), ()))

    def dot(a, b):
        return lax.dot_general(a, b, dims, preferred_element_type=jnp.float32)

    return dot(left[0], right[0]) + (dot(left[0], right[1]) + dot(left[1], right[0]))


def kernel(
    n, g_ref, c_ref, f_ref, cov_ref, grad_ref,
    g_in, c_in, c_odd, cov_in, grad_buf, sum_in, sum_out, d_half, k_half, s_half,
    lag_odd, sigma_odd, ge, go, a, f, e, l_half, v_half,
    pair_send, pair_recv, top_send, top_recv, late_send, late_recv, down_send, down_recv, side_send, side_recv,
    sum_send, sum_recv, up_send, up_recv, share_send, share_recv,
):
    width = f_ref.shape[0]
    half = width // 2
    rows = width // CHUNKS
    me = lax.axis_index("tm")
    side, pair, pairs = me % 2, me // 2, n // 2
    is_even, is_odd = side == 0, side == 1
    partner, up, down = me + 1 - 2 * side, me + 2, me - 2
    has_up, has_down = pair < pairs - 1, pair > 0
    mine = pl.ds(pl.multiple_of(side * half, half), half)
    other = pl.ds(pl.multiple_of((1 - side) * half, half), half)

    def chunk(r):
        return pl.ds(r * rows, rows)

    sends = CHUNKS * PIECES

    def piece(t):
        return pl.ds(t * (width // sends), width // sends)

    def pieces(r):
        return range(r * PIECES, (r + 1) * PIECES)

    def remote(src, dst, send, recv, device):
        return pltpu.make_async_remote_copy(
            src_ref=src, dst_ref=dst, send_sem=send, recv_sem=recv,
            device_id={"tm": device}, device_id_type=pl.DeviceIdType.MESH,
        )

    def get(pair_ref, *index):
        return pair_ref[(0, *index)], pair_ref[(1, *index)]

    def put(pair_ref, value, *index):
        high, low = split(value)
        pair_ref[(0, *index)] = high
        pair_ref[(1, *index)] = low

    every = slice(None)

    barrier = pltpu.get_barrier_semaphore()

    def greet(device):
        pl.semaphore_signal(
            barrier, inc=1, device_id={"tm": device}, device_id_type=pl.DeviceIdType.MESH
        )

    greet(partner)
    pl.when(has_up)(lambda: greet(up))
    pl.when(has_down)(lambda: greet(down))
    pl.semaphore_wait(barrier, 1 + has_up.astype(jnp.int32) + has_down.astype(jnp.int32))

    is_top = jnp.logical_not(has_up)
    low, high = pl.ds(0, half), pl.ds(half, half)

    def swap(i, ref, target, *index):
        return remote(
            ref.at[(0, *index)], target.at[index], pair_send.at[i], pair_recv.at[i], partner
        )

    send_g = remote(g_ref.at[0], g_in, pair_send.at[0], pair_recv.at[0], partner)
    send_c_low = swap(1, c_ref, c_in, low)
    send_c_high = swap(2, c_ref, c_in, high, high)
    send_c_half = swap(1, c_ref, c_in, every, high)

    @pl.when(is_odd)
    def _():
        pl.when(has_up)(send_g.start)
        send_c_low.start()
        send_c_high.start()

    @pl.when(is_even & has_up)
    def _():
        send_g.start()
        send_c_half.start()

    def receive_c_odd():
        send_c_low.wait_recv()
        send_c_high.wait_recv()
        c_odd[low] = c_in[low]
        c_odd[high, half:] = c_in[high, half:]
        c_odd[high, :half] = c_in[low, half:].T

    def send_down(t):
        return remote(
            s_half.at[piece(t)], cov_in.at[side, piece(t)], down_send.at[t], down_recv.at[t], down
        )

    def send_side(t):
        return remote(
            cov_in.at[side, piece(t)], cov_in.at[side, piece(t)],
            side_send.at[t], side_recv.at[t], partner,
        )

    second = pair == pairs - 2
    late = range(sends // 2, sends)

    def forwards(t):
        if t in late:
            return jnp.logical_not(second)
        return is_even | jnp.logical_not(second)

    def send_late(t):
        return remote(
            s_half.at[piece(t)], d_half.at[piece(t)], late_send.at[t], late_recv.at[t], partner
        )

    def send_top(t):
        return remote(
            d_half.at[piece(t)], s_half.at[piece(t)], top_send.at[t], top_recv.at[t], partner
        )

    def send_other_down(t):
        return remote(
            d_half.at[piece(t)], cov_in.at[1 - side, piece(t)], side_send.at[t], side_recv.at[t], down
        )

    @pl.when(is_even)
    def _():
        put(ge, g_ref[0], every, every)

    @pl.when(is_odd)
    def _():
        c_odd[...] = c_ref[0]

    @pl.when(is_top)
    def _():
        e[...] = jnp.zeros_like(e)
        go[...] = jnp.zeros_like(go)
        l_half[...] = jnp.zeros_like(l_half)
        lag_odd[...] = jnp.zeros_like(lag_odd)

    @pl.when(is_top & is_even)
    def _():
        receive_c_odd()
        k_all = product(split(c_odd[...]), get(ge, every, every), True)
        k_half[...] = k_all[:, :half]
        put(e, k_all, every, every)
        for r in range(CHUNKS):
            q = chunk(r)
            sigma = product(get(ge, q, every), get(e, every, every)) + c_ref[0, q]
            s_half[q] = sigma[:, :half]
            d_half[q] = sigma[:, half:]
            for t in pieces(r):
                send_top(t).start()
                if t in late:
                    send_late(t).start()
                pl.when(has_down)(send_down(t).start)
                pl.when(has_down)(send_other_down(t).start)
        send_g.start()
        e[...] = jnp.zeros_like(e)

    put(f, f_ref[...], every, every)

    @pl.when(is_top & is_odd)
    def _():
        for t in range(sends):
            send_top(t).wait_recv()
            pl.when(has_down)(send_down(t).start)
            if t in late:
                send_late(t).wait_recv()
                pl.when(has_down)(send_other_down(t).start)
        send_g.wait_recv()
        put(ge, g_in[...], every, every)
        k_half[...] = product(split(c_odd[...]), get(ge, mine, every), True)

    @pl.when(has_up)
    def _():
        @pl.when(is_even)
        def _():
            send_g.wait_recv()
            put(go, g_in[...], every, every)

        @pl.when(is_odd)
        def _():
            put(go, g_ref[0], every, every)
            send_g.wait_recv()
            put(ge, g_in[...], every, every)

        put(a, product(get(ge, every, every), get(go, every, every)), every, every)
        pl.when(is_even)(receive_c_odd)
        k_value = product(split(c_odd[...]), get(ge, mine, every), True)
        k_half[...] = k_value
        d_half[...] = product(get(ge, every, every), split(k_value))

        @pl.when(is_even)
        def _():
            d_half[...] += c_ref[0, :, :half]

        @pl.when(is_odd)
        def _():
            send_c_half.wait_recv()
            d_half[...] += c_in[:, half:]

        def use(r):
            q = chunk(r)
            for t in pieces(r):
                send_side(t).wait_recv()
            put(e, cov_in[0, q], q, slice(0, half))
            put(e, cov_in[1, q], q, slice(half, width))
            rows_of_e = get(e, q, every)
            put(l_half, product(rows_of_e, get(a, mine, every), True), q, every)

            @pl.when(jnp.logical_not(has_down))
            def _():
                lag_odd[q] = product(rows_of_e, get(go, mine, every), True)

        used = 0
        for t in range(sends):
            send_down(t).wait_recv()
            pl.when(forwards(t))(send_side(t).start)
            if t % PIECES == 0 and t >= 2 * PIECES:
                use(used)
                used += 1
        for r in range(used, CHUNKS):
            use(r)
        for r in range(CHUNKS):
            q = chunk(r)
            s_half[q] = product(get(a, q, every), get(l_half, every, every)) + d_half[q]
            for t in pieces(r):
                pl.when(has_down)(send_down(t).start)

        @pl.when(has_down)
        def _():
            lag_odd[...] = product(get(e, every, every), get(go, mine, every), True)

    sigma_odd[...] = product(get(go, every, every), split(lag_odd[...]))

    @pl.when(is_even)
    def _():
        sigma_odd[...] += c_odd[:, :half]

    @pl.when(is_odd)
    def _():
        own = sigma_odd[...] + c_odd[:, half:]
        sigma_odd[...] = own
        cov_ref[0, :, half:] = own

    counted = jnp.where(has_up, 1.0, 0.0).astype(jnp.float32)
    put(v_half, counted * sigma_odd[...] + s_half[...], every, every)

    def send_sum(r):
        return remote(
            sum_out.at[chunk(r)], sum_in.at[chunk(r)], sum_send.at[r], sum_recv.at[r], down
        )

    def send_up(r):
        return remote(
            grad_buf.at[side, piece(r)], grad_buf.at[side, piece(r)],
            up_send.at[r], up_recv.at[r], up,
        )

    def share(r):
        return remote(
            grad_buf.at[side, piece(r)], grad_buf.at[side, piece(r)],
            share_send.at[r], share_recv.at[r], partner,
        )

    for r in range(CHUNKS):
        q = chunk(r)
        sum_out[q] = (
            lag_odd[q]
            + (product(get(go, q, every), get(l_half, every, every)) + k_half[q])
            - product(get(f, q, every), get(v_half, every, every))
        )

        @pl.when(has_up)
        def _():
            send_sum(r).wait_recv()
            sum_out[q] += sum_in[q]

        pl.when(has_down)(send_sum(r).start)

        @pl.when(jnp.logical_not(has_down))
        def _():
            grad_buf[side, q] = sum_out[q] / (n - 1)
            for t in pieces(r):
                pl.when(has_up)(send_up(t).start)
                share(t).start()

    @pl.when(is_even)
    def _():
        cov_ref[0, :, :half] = s_half[...]
        k_other = product(split(c_odd[...]), get(ge, other, every), True)
        cov_ref[0, :, half:] = (
            product(get(ge, every, every), split(k_other)) + c_ref[0, :, half:]
        )

        @pl.when(has_up)
        def _():
            l_other = product(get(e, every, every), get(a, other, every), True)
            cov_ref[0, :, half:] += product(get(a, every, every), split(l_other))

    @pl.when(is_odd)
    def _():
        l_other = product(get(e, every, every), get(go, other, every), True)
        cov_ref[0, :, :half] = (
            product(get(go, every, every), split(l_other)) + c_odd[:, :half]
        )

    @pl.when(has_down)
    def _():
        for r in range(sends):
            send_up(r).wait_recv()
            pl.when(has_up)(send_up(r).start)
            share(r).start()

    for r in range(sends):
        share(r).wait_recv()
        grad_ref[piece(r), :half] = grad_buf[0, piece(r)]
        grad_ref[piece(r), half:] = grad_buf[1, piece(r)]

    pl.when(has_up | is_even)(send_g.wait_send)
    pl.when(is_odd)(send_c_low.wait_send)
    pl.when(is_odd)(send_c_high.wait_send)
    pl.when(has_up & is_even)(send_c_half.wait_send)
    for r in range(CHUNKS):
        pl.when(has_down)(send_sum(r).wait_send)
    for r in range(sends):
        pl.when(has_down)(send_down(r).wait_send)
        pl.when(has_up & forwards(r))(send_side(r).wait_send)
        pl.when(is_top & is_even)(send_top(r).wait_send)
        pl.when(is_top & is_even & has_down)(send_other_down(r).wait_send)
        if r in late:
            pl.when(is_top & is_even)(send_late(r).wait_send)
            pl.when(is_top & is_odd & has_down)(send_other_down(r).wait_send)
        pl.when(has_up)(send_up(r).wait_send)
        share(r).wait_send()


def on_device(n, transitions, cond_covs, transition_est):
    width = transitions.shape[1]
    half = width // 2
    f32, b16 = jnp.float32, jnp.bfloat16
    vmem = pl.BlockSpec(memory_space=pltpu.VMEM)
    whole, column_half = (width, width), (width, half)
    dma = pltpu.SemaphoreType.DMA
    sends = CHUNKS * PIECES
    return pl.pallas_call(
        functools.partial(kernel, n),
        out_shape=(
            jax.ShapeDtypeStruct(transitions.shape, f32),
            jax.ShapeDtypeStruct(transition_est.shape, f32),
        ),
        in_specs=[vmem] * 3,
        out_specs=(vmem, vmem),
        scratch_shapes=[
            *[pltpu.VMEM(whole, f32)] * 3,
            *[pltpu.VMEM((2, *column_half), f32)] * 2,
            *[pltpu.VMEM(column_half, f32)] * 7,
            *[pltpu.VMEM((2, *whole), b16)] * 5,
            *[pltpu.VMEM((2, *column_half), b16)] * 2,
            *[dma((3,))] * 2,
            *[dma((sends,))] * 8,
            *[dma((CHUNKS,))] * 2,
            *[dma((sends,))] * 4,
        ],
        compiler_params=pltpu.CompilerParams(
            collective_id=0, has_side_effects=True, vmem_limit_bytes=56 * 2**20
        ),
    )(transitions, cond_covs, transition_est)


def solution(mesh):
    return jax.shard_map(
        functools.partial(on_device, mesh.shape["tm"]),
        mesh=mesh,
        in_specs=(P(("rep", "tm"), None, None), P(("rep", "tm"), None, None), P("rep", None)),
        out_specs=(P(("rep", "tm"), None, None), P("rep", None)),
        check_vma=False,
    )
```

```python
import functools

import jax
import jax.numpy as jnp
from jax import lax
from jax.experimental import pallas as pl
from jax.experimental.pallas import tpu as pltpu
from jax.sharding import PartitionSpec as P

CHUNKS = 4
PIECES = 4


def split(value):
    high = value.astype(jnp.bfloat16)
    low = (value - high.astype(jnp.float32)).astype(jnp.bfloat16)
    return high, low


def product(left, right, transposed=False):
    dims = (((1,), (1 if transposed else 0,)), ((), ()))

    def dot(a, b):
        return lax.dot_general(a, b, dims, preferred_element_type=jnp.float32)

    return dot(left[0], right[0]) + (dot(left[0], right[1]) + dot(left[1], right[0]))


def kernel(
    n, g_ref, c_ref, f_ref, cov_ref, grad_ref,
    g_in, c_in, c_odd, cov_in, grad_buf, sum_in, sum_out, d_half, k_half, s_half,
    lag_odd, sigma_odd, ge, go, a, f, e, l_half, v_half,
    pair_send, pair_recv, top_send, top_recv, late_send, late_recv, down_send, down_recv, side_send, side_recv,
    sum_send, sum_recv, up_send, up_recv, share_send, share_recv,
):
    width = f_ref.shape[0]
    half = width // 2
    rows = width // CHUNKS
    me = lax.axis_index("tm")
    side, pair, pairs = me % 2, me // 2, n // 2
    is_even, is_odd = side == 0, side == 1
    partner, up, down = me + 1 - 2 * side, me + 2, me - 2
    has_up, has_down = pair < pairs - 1, pair > 0
    mine = pl.ds(pl.multiple_of(side * half, half), half)
    other = pl.ds(pl.multiple_of((1 - side) * half, half), half)

    def chunk(r):
        return pl.ds(r * rows, rows)

    sends = CHUNKS * PIECES

    def piece(t):
        return pl.ds(t * (width // sends), width // sends)

    def pieces(r):
        return range(r * PIECES, (r + 1) * PIECES)

    def remote(src, dst, send, recv, device):
        return pltpu.make_async_remote_copy(
            src_ref=src, dst_ref=dst, send_sem=send, recv_sem=recv,
            device_id={"tm": device}, device_id_type=pl.DeviceIdType.MESH,
        )

    def get(pair_ref, *index):
        return pair_ref[(0, *index)], pair_ref[(1, *index)]

    def put(pair_ref, value, *index):
        high, low = split(value)
        pair_ref[(0, *index)] = high
        pair_ref[(1, *index)] = low

    every = slice(None)

    barrier = pltpu.get_barrier_semaphore()

    def greet(device):
        pl.semaphore_signal(
            barrier, inc=1, device_id={"tm": device}, device_id_type=pl.DeviceIdType.MESH
        )

    greet(partner)
    pl.when(has_up)(lambda: greet(up))
    pl.when(has_down)(lambda: greet(down))
    pl.semaphore_wait(barrier, 1 + has_up.astype(jnp.int32) + has_down.astype(jnp.int32))

    is_top = jnp.logical_not(has_up)
    low, high = pl.ds(0, half), pl.ds(half, half)

    def swap(i, ref, target, *index):
        return remote(
            ref.at[(0, *index)], target.at[index], pair_send.at[i], pair_recv.at[i], partner
        )

    send_g = remote(g_ref.at[0], g_in, pair_send.at[0], pair_recv.at[0], partner)
    send_c_low = swap(1, c_ref, c_in, low)
    send_c_high = swap(2, c_ref, c_in, high, high)
    send_c_half = swap(1, c_ref, c_in, every, high)

    @pl.when(is_odd)
    def _():
        pl.when(has_up)(send_g.start)
        send_c_low.start()
        send_c_high.start()

    @pl.when(is_even & has_up)
    def _():
        send_g.start()
        send_c_half.start()

    def receive_c_odd():
        send_c_low.wait_recv()
        send_c_high.wait_recv()
        c_odd[low] = c_in[low]
        c_odd[high, half:] = c_in[high, half:]
        c_odd[high, :half] = c_in[low, half:].T

    def send_down(t):
        return remote(
            s_half.at[piece(t)], cov_in.at[side, piece(t)], down_send.at[t], down_recv.at[t], down
        )

    def send_side(t):
        return remote(
            cov_in.at[side, piece(t)], cov_in.at[side, piece(t)],
            side_send.at[t], side_recv.at[t], partner,
        )

    second = pair == pairs - 2
    late = range(sends // 2, sends)
    ahead = second & is_even

    def forwards(t):
        if t in late:
            return jnp.logical_not(second)
        return is_even | jnp.logical_not(second)

    def send_late(t):
        return remote(
            s_half.at[piece(t)], d_half.at[piece(t)], late_send.at[t], late_recv.at[t], partner
        )

    def send_top(t):
        return remote(
            d_half.at[piece(t)], s_half.at[piece(t)], top_send.at[t], top_recv.at[t], partner
        )

    def send_other_down(t):
        return remote(
            d_half.at[piece(t)], cov_in.at[1 - side, piece(t)], side_send.at[t], side_recv.at[t], down
        )

    @pl.when(is_even)
    def _():
        put(ge, g_ref[0], every, every)

    @pl.when(is_odd)
    def _():
        c_odd[...] = c_ref[0]

    @pl.when(is_top)
    def _():
        e[...] = jnp.zeros_like(e)
        go[...] = jnp.zeros_like(go)
        l_half[...] = jnp.zeros_like(l_half)
        lag_odd[...] = jnp.zeros_like(lag_odd)

    @pl.when(is_top & is_even)
    def _():
        receive_c_odd()
        k_all = product(split(c_odd[...]), get(ge, every, every), True)
        k_half[...] = k_all[:, :half]
        put(e, k_all, every, every)
        for r in range(CHUNKS):
            q = chunk(r)
            sigma = product(get(ge, q, every), get(e, every, every)) + c_ref[0, q]
            s_half[q] = sigma[:, :half]
            d_half[q] = sigma[:, half:]
            for t in pieces(r):
                send_top(t).start()
                if t in late:
                    send_late(t).start()
                pl.when(has_down)(send_down(t).start)
                pl.when(has_down)(send_other_down(t).start)
        send_g.start()
        e[...] = jnp.zeros_like(e)

    put(f, f_ref[...], every, every)

    @pl.when(is_top & is_odd)
    def _():
        for t in range(sends):
            send_top(t).wait_recv()
            pl.when(has_down)(send_down(t).start)
            if t in late:
                send_late(t).wait_recv()
                pl.when(has_down)(send_other_down(t).start)
        send_g.wait_recv()
        put(ge, g_in[...], every, every)
        k_half[...] = product(split(c_odd[...]), get(ge, mine, every), True)

    @pl.when(has_up)
    def _():
        @pl.when(is_even)
        def _():
            send_g.wait_recv()
            put(go, g_in[...], every, every)

        @pl.when(is_odd)
        def _():
            put(go, g_ref[0], every, every)
            send_g.wait_recv()
            put(ge, g_in[...], every, every)

        put(a, product(get(ge, every, every), get(go, every, every)), every, every)

        @pl.when(ahead)
        def _():
            for t in range(sends // 2):
                send_down(t).wait_recv()
                send_side(t).start()

        pl.when(is_even)(receive_c_odd)
        k_value = product(split(c_odd[...]), get(ge, mine, every), True)
        k_half[...] = k_value
        d_half[...] = product(get(ge, every, every), split(k_value))

        @pl.when(is_even)
        def _():
            d_half[...] += c_ref[0, :, :half]

        @pl.when(is_odd)
        def _():
            send_c_half.wait_recv()
            d_half[...] += c_in[:, half:]

        def use(r):
            q = chunk(r)
            for t in pieces(r):
                send_side(t).wait_recv()
            put(e, cov_in[0, q], q, slice(0, half))
            put(e, cov_in[1, q], q, slice(half, width))
            rows_of_e = get(e, q, every)
            put(l_half, product(rows_of_e, get(a, mine, every), True), q, every)

            @pl.when(jnp.logical_not(has_down))
            def _():
                lag_odd[q] = product(rows_of_e, get(go, mine, every), True)

        used = 0
        for t in range(sends):
            if t in late:
                send_down(t).wait_recv()
                pl.when(forwards(t))(send_side(t).start)
            else:
                pl.when(jnp.logical_not(ahead))(send_down(t).wait_recv)
                pl.when(jnp.logical_not(second))(send_side(t).start)
            if t % PIECES == 0 and t >= 2 * PIECES:
                use(used)
                used += 1
        for r in range(used, CHUNKS):
            use(r)
        for r in range(CHUNKS):
            q = chunk(r)
            s_half[q] = product(get(a, q, every), get(l_half, every, every)) + d_half[q]
            for t in pieces(r):
                pl.when(has_down)(send_down(t).start)

        @pl.when(has_down)
        def _():
            lag_odd[...] = product(get(e, every, every), get(go, mine, every), True)

    sigma_odd[...] = product(get(go, every, every), split(lag_odd[...]))

    @pl.when(is_even)
    def _():
        sigma_odd[...] += c_odd[:, :half]

    @pl.when(is_odd)
    def _():
        own = sigma_odd[...] + c_odd[:, half:]
        sigma_odd[...] = own
        cov_ref[0, :, half:] = own

    counted = jnp.where(has_up, 1.0, 0.0).astype(jnp.float32)
    put(v_half, counted * sigma_odd[...] + s_half[...], every, every)

    def send_sum(r):
        return remote(
            sum_out.at[chunk(r)], sum_in.at[chunk(r)], sum_send.at[r], sum_recv.at[r], down
        )

    def send_up(r):
        return remote(
            grad_buf.at[side, piece(r)], grad_buf.at[side, piece(r)],
            up_send.at[r], up_recv.at[r], up,
        )

    def share(r):
        return remote(
            grad_buf.at[side, piece(r)], grad_buf.at[side, piece(r)],
            share_send.at[r], share_recv.at[r], partner,
        )

    for r in range(CHUNKS):
        q = chunk(r)
        sum_out[q] = (
            lag_odd[q]
            + (product(get(go, q, every), get(l_half, every, every)) + k_half[q])
            - product(get(f, q, every), get(v_half, every, every))
        )

        @pl.when(has_up)
        def _():
            send_sum(r).wait_recv()
            sum_out[q] += sum_in[q]

        pl.when(has_down)(send_sum(r).start)

        @pl.when(jnp.logical_not(has_down))
        def _():
            grad_buf[side, q] = sum_out[q] / (n - 1)
            for t in pieces(r):
                pl.when(has_up)(send_up(t).start)
                share(t).start()

    @pl.when(is_even)
    def _():
        cov_ref[0, :, :half] = s_half[...]
        k_other = product(split(c_odd[...]), get(ge, other, every), True)
        cov_ref[0, :, half:] = (
            product(get(ge, every, every), split(k_other)) + c_ref[0, :, half:]
        )

        @pl.when(has_up)
        def _():
            l_other = product(get(e, every, every), get(a, other, every), True)
            cov_ref[0, :, half:] += product(get(a, every, every), split(l_other))

    @pl.when(is_odd)
    def _():
        l_other = product(get(e, every, every), get(go, other, every), True)
        cov_ref[0, :, :half] = (
            product(get(go, every, every), split(l_other)) + c_odd[:, :half]
        )

    @pl.when(has_down)
    def _():
        for r in range(sends):
            send_up(r).wait_recv()
            pl.when(has_up)(send_up(r).start)
            share(r).start()

    for r in range(sends):
        share(r).wait_recv()
        grad_ref[piece(r), :half] = grad_buf[0, piece(r)]
        grad_ref[piece(r), half:] = grad_buf[1, piece(r)]

    pl.when(has_up | is_even)(send_g.wait_send)
    pl.when(is_odd)(send_c_low.wait_send)
    pl.when(is_odd)(send_c_high.wait_send)
    pl.when(has_up & is_even)(send_c_half.wait_send)
    for r in range(CHUNKS):
        pl.when(has_down)(send_sum(r).wait_send)
    for r in range(sends):
        pl.when(has_down)(send_down(r).wait_send)
        pl.when(has_up & forwards(r))(send_side(r).wait_send)
        pl.when(is_top & is_even)(send_top(r).wait_send)
        pl.when(is_top & is_even & has_down)(send_other_down(r).wait_send)
        if r in late:
            pl.when(is_top & is_even)(send_late(r).wait_send)
            pl.when(is_top & is_odd & has_down)(send_other_down(r).wait_send)
        pl.when(has_up)(send_up(r).wait_send)
        share(r).wait_send()


def on_device(n, transitions, cond_covs, transition_est):
    width = transitions.shape[1]
    half = width // 2
    f32, b16 = jnp.float32, jnp.bfloat16
    vmem = pl.BlockSpec(memory_space=pltpu.VMEM)
    whole, column_half = (width, width), (width, half)
    dma = pltpu.SemaphoreType.DMA
    sends = CHUNKS * PIECES
    return pl.pallas_call(
        functools.partial(kernel, n),
        out_shape=(
            jax.ShapeDtypeStruct(transitions.shape, f32),
            jax.ShapeDtypeStruct(transition_est.shape, f32),
        ),
        in_specs=[vmem] * 3,
        out_specs=(vmem, vmem),
        scratch_shapes=[
            *[pltpu.VMEM(whole, f32)] * 3,
            *[pltpu.VMEM((2, *column_half), f32)] * 2,
            *[pltpu.VMEM(column_half, f32)] * 7,
            *[pltpu.VMEM((2, *whole), b16)] * 5,
            *[pltpu.VMEM((2, *column_half), b16)] * 2,
            *[dma((3,))] * 2,
            *[dma((sends,))] * 8,
            *[dma((CHUNKS,))] * 2,
            *[dma((sends,))] * 4,
        ],
        compiler_params=pltpu.CompilerParams(
            collective_id=0, has_side_effects=True, vmem_limit_bytes=56 * 2**20
        ),
    )(transitions, cond_covs, transition_est)


def solution(mesh):
    return jax.shard_map(
        functools.partial(on_device, mesh.shape["tm"]),
        mesh=mesh,
        in_specs=(P(("rep", "tm"), None, None), P(("rep", "tm"), None, None), P("rep", None)),
        out_specs=(P(("rep", "tm"), None, None), P("rep", None)),
        check_vma=False,
    )
```
